256 devices in a mesh: row: 16 (over x, y_hi, core), col: 16 (over z, y_lo).
Axes of the slice: x: 4, y: 4 (y_hi: 2, y_lo: 2; y = y_hi * 2 + y_lo), z: 8, core: 2. Of those that a mesh axis runs over, the one named last changes fastest.
Arguments:
- p_cols: int32 [256, 64], P('row', 'col'), may hold values from -1 to 15, as said below
- p_data: float32 [16384, 4096], P('row', 'col'), may hold values from -1.5 to 1.5
Outputs:
- product: float32 [16384, 16384], P('row', 'col')
The draws below stay inside these ranges and needn't reach their ends.
Inputs may be any that keep to these rules, and one draw needn't show every extreme that they name: `p_cols`: in each column tile, each block row has 1 to 4 used slots, the used ones first, with distinct columns; the first block row of each device's rows has all 4 used.
All inputs are finite; a program needn't handle non-finite values.
Results may differ from the reference program's by a relative error of at most 0.0003.
Values sent between devices are 32-bit elements; how exact they have to be, the bound alone decides.
A program may use at most 192 MiB of HBM per device.

```python
import jax
import jax.numpy as jnp
from jax import lax

BS = 64
W = 4
RB = 16
STEPS = 4
RATIO = 1
CB = 16
NB = 256
N_ROW = 16
N_COL = 16


def draw_p_cols(key, part):
    score_key = jax.random.fold_in(key, 11)
    count_key = jax.random.fold_in(key, 23)
    scores = jax.random.randint(score_key, (NB, N_COL, CB), 0, 1 << 20, dtype=jnp.int32)
    scores = scores * CB + jnp.arange(CB, dtype=jnp.int32)
    chosen = lax.top_k(scores, W)[1].astype(jnp.int32)
    counts = jax.random.randint(count_key, (NB, N_COL), 1, W + 1, dtype=jnp.int32)
    first_rows = jnp.arange(NB, dtype=jnp.int32) % RB == 0
    counts = jnp.where(first_rows[:, None], W, counts)
    used = jnp.arange(W, dtype=jnp.int32)[None, None, :] < counts[:, :, None]
    filled = jnp.where(used, chosen, -1)
    return filled.reshape(NB, N_COL * W).astype(jnp.int32)


def steps_of(key, dims, cuts, least, largest):
    level, own = 1.0, jax.random.fold_in(key, 6)
    for dim, blocks in cuts:
        heights = jnp.exp(jax.random.uniform(jax.random.fold_in(own, dim), (blocks,), jnp.float32, least / len(cuts), largest / len(cuts)))
        level = level * jnp.repeat(heights, dims[dim] // blocks).reshape([-1 if axis == dim else 1 for axis in range(len(dims))])
    return level


def noise(rng, dims, width, limit, pieces=(), kind=jnp.bfloat16):
    values = width * jax.random.normal(rng, dims, jnp.float32)
    if pieces:
        values = values * steps_of(rng, dims, pieces, -0.22, 0.18)
    return jnp.clip(values, -limit, limit).astype(kind)


def setup_inputs(seed: int = 0) -> dict:
    splits = jax.random.split(jax.random.key(seed), 3)
    p_cols = draw_p_cols(jax.random.fold_in(splits[2], 71), 0)
    p_data = noise(splits[1], (NB * BS, N_COL * W * BS), 0.25, 1.5, ((0, 16), (1, 16)), jnp.float32)
    return {"p_cols": p_cols, "p_data": p_data}


def tile_product(left_cols, left_data, right_cols, right_data, piece_index, block_rows, tile_cols):
    slot_count = left_cols.shape[1]
    inner_local = left_cols - piece_index * block_rows
    usable = (left_cols >= 0) & (inner_local >= 0) & (inner_local < block_rows)
    inner_row = jnp.clip(inner_local, 0, block_rows - 1).astype(jnp.int32)
    left_blocks = left_data.reshape(block_rows, BS, slot_count, BS).transpose(0, 2, 1, 3)
    left_blocks = jnp.where(usable[:, :, None, None], left_blocks, jnp.zeros_like(left_blocks))
    right_rows = right_data.reshape(block_rows, BS, slot_count * BS)[inner_row]
    targets = right_cols[inner_row]
    partial_prod = jnp.einsum("rwij,rwjk->rwik", left_blocks, right_rows, precision=lax.Precision.HIGHEST)
    partial_prod = partial_prod.reshape(block_rows, slot_count, BS, slot_count, BS)
    placing = (targets[..., None] == jnp.arange(tile_cols, dtype=jnp.int32)).astype(left_data.dtype)
    result = jnp.einsum("rwvc,rwivk->rick", placing, partial_prod, precision=lax.Precision.HIGHEST)
    return result.reshape(block_rows * BS, tile_cols * BS)


def reference(p_cols, p_data):
    def one_tile(tile_index):
        row_tile = tile_index // N_COL
        col_tile = tile_index % N_COL
        accum = jnp.zeros((RB * BS, CB * BS), p_data.dtype)
        for step_index in range(STEPS):
            inner_tile = (row_tile + RATIO * col_tile + step_index) % N_ROW
            left_tile_col = inner_tile // RATIO
            piece_index = inner_tile % RATIO
            left_cols = lax.dynamic_slice(p_cols, ((row_tile * RB).astype(jnp.int32), (left_tile_col * W).astype(jnp.int32)), (RB, W))
            left_data = lax.dynamic_slice(p_data, ((row_tile * RB * BS).astype(jnp.int32), (left_tile_col * W * BS).astype(jnp.int32)), (RB * BS, W * BS))
            right_cols = lax.dynamic_slice(p_cols, ((inner_tile * RB).astype(jnp.int32), (col_tile * W).astype(jnp.int32)), (RB, W))
            right_data = lax.dynamic_slice(p_data, ((inner_tile * RB * BS).astype(jnp.int32), (col_tile * W * BS).astype(jnp.int32)), (RB * BS, W * BS))
            accum = accum + tile_product(left_cols, left_data, right_cols, right_data, piece_index, RB, CB)
        return accum

    stacked = lax.map(one_tile, jnp.arange(N_ROW * N_COL, dtype=jnp.int32))
    stacked = stacked.reshape(N_ROW, N_COL, RB * BS, CB * BS).transpose(0, 2, 1, 3)
    return stacked.reshape(NB * BS, N_COL * CB * BS)
```

```python
import functools

import jax
import jax.numpy as jnp
from jax import lax
from jax.experimental import pallas as pl
from jax.experimental.pallas import tpu as pltpu
from jax.sharding import PartitionSpec as P

BS = 64
STEPS = 4
ROWS = 1032
CHUNKS = ((0, 256), (256, 256), (512, 256), (768, 264))
MESH = pl.DeviceIdType.MESH


def gather_kernel(data_ref, cols_ref, left_ref, right_ref, own, load_sem, keep_sem, send_sem, left_sem, right_sem):
    row, col = lax.axis_index("row"), lax.axis_index("col")
    q, core = row // 2, row % 2
    half = q % 2
    z, y = col // 2, col % 2
    odd = z % 2

    def at(q_new, z_new, y_new, core_new):
        return (2 * ((q_new + 32) % 8) + core_new, 2 * ((z_new + 32) % 8) + y_new)

    depth = q + core
    land = jnp.where((depth >= 5) & (depth <= 7) | (depth >= 3) & (depth <= 4) & (core == 1), 1, 0)
    skew = depth + land
    left_own = skew % 8 == 0
    lane = 2 * land - 1
    near_slot = lambda index: 2 * index + core
    cross_slot = lambda index: 2 * index + 1 - core
    shift = core + y - 1
    straight = shift == 0
    passes = y != core
    pass_lane = 2 * core - 1

    first = jnp.where(odd == 1, 1, jnp.where(z < 4, 0, 2))
    right_own = (z + first) % 8 == 0
    second = jnp.where(odd == 1, 2 - 2 * half, 2 - first)
    third = 3 - first - second
    own_slot = lambda index: (2 * index - y + 5) % 5
    hop = jnp.where(half == 1, -1, 1)
    send1_to = q + jnp.where(odd == 1, hop, 2 * first - 2)
    send1_as = jnp.where(odd == 1, 1 - hop, 2 - first)
    send2_of = jnp.where(odd == 1, second, 2 - 2 * half)
    send2_to = q + jnp.where(odd == 1, 2 * hop, hop)
    send2_as = jnp.where(odd == 1, third, 1)

    barrier = pltpu.get_barrier_semaphore()

    def greet(device):
        pl.semaphore_signal(barrier, inc=1, device_id=device, device_id_type=MESH)

    @pl.when(jnp.logical_not(left_own))
    def _():
        greet(at(q, z + skew, y, core))

    greet(at(q, z - lane, y, core))
    greet(at(q, z, 1 - y, core))

    @pl.when(passes)
    def _():
        greet(at(q, z - pass_lane, y, core))

    @pl.when(jnp.logical_not(right_own))
    def _():
        greet(at(q + z + first, z, y, core))

    greet(at(q + jnp.where(odd == 1, hop, 2 - 2 * first), z, y, core))
    greet(at(q + jnp.where(odd == 1, -2 * hop, hop), z, y, core))
    greet(at(q, z, y, 1 - core))

    load = pltpu.make_async_copy(data_ref, own.at[pl.ds(0, 1024)], load_sem.at[0])
    load_cols = pltpu.make_async_copy(cols_ref, own.at[pl.ds(1024, 8)], load_sem.at[1])
    load.start()
    load_cols.start()
    load.wait()
    load_cols.wait()
    absent = left_own.astype(jnp.int32) + right_own.astype(jnp.int32) + jnp.where(passes, 0, 1)
    pl.semaphore_wait(barrier, 8 - absent)

    def move(source, target, kind, chunk, sem, device):
        return pltpu.make_async_remote_copy(
            src_ref=source,
            dst_ref=target,
            send_sem=send_sem.at[kind, chunk],
            recv_sem=sem,
            device_id=device,
            device_id_type=MESH,
        )

    def part(ref, slot, chunk):
        start, size = CHUNKS[chunk]
        return ref.at[slot, pl.ds(start, size)]

    def own_part(chunk):
        start, size = CHUNKS[chunk]
        return own.at[pl.ds(start, size)]

    def left_skew(chunk):
        slot = near_slot(land)
        return move(own_part(chunk), part(left_ref, slot, chunk), 0, chunk, left_sem.at[slot, chunk], at(q, z - skew, y, core))

    def left_next(chunk):
        slot = near_slot(1 - land)
        return move(part(left_ref, near_slot(land), chunk), part(left_ref, slot, chunk), 1, chunk, left_sem.at[slot, chunk], at(q, z + lane, y, core))

    def left_cross(index, kind, chunk):
        slot = cross_slot(index + shift)
        return move(part(left_ref, near_slot(index), chunk), part(left_ref, slot, chunk), kind, chunk, left_sem.at[slot, chunk], at(q, z, 1 - y, core))

    def left_pass(chunk):
        slot = cross_slot(1 - core)
        return move(part(left_ref, cross_slot(core), chunk), part(left_ref, slot, chunk), 4, chunk, left_sem.at[slot, chunk], at(q, z + pass_lane, y, core))

    def right_skew(chunk):
        slot = own_slot(first)
        return move(own_part(chunk), part(right_ref, slot, chunk), 5, chunk, right_sem.at[slot, chunk], at(q - z - first, z, y, core))

    def right_send1(chunk):
        slot = own_slot(send1_as)
        return move(part(right_ref, own_slot(first), chunk), part(right_ref, slot, chunk), 6, chunk, right_sem.at[slot, chunk], at(send1_to, z, y, core))

    def right_send2(chunk):
        slot = own_slot(send2_as)
        return move(part(right_ref, own_slot(send2_of), chunk), part(right_ref, slot, chunk), 7, chunk, right_sem.at[slot, chunk], at(send2_to, z, y, core))

    def right_share(index, kind, chunk):
        slot = 2 * index - 1 + 2 * core - y
        return move(part(right_ref, own_slot(index), chunk), part(right_ref, slot, chunk), kind, chunk, right_sem.at[slot, chunk], at(q, z, y, 1 - core))

    def left_here(slot, chunk):
        move(part(left_ref, slot, chunk), part(left_ref, slot, chunk), 0, chunk, left_sem.at[slot, chunk], at(q, z, 1 - y, core)).wait_recv()

    def right_here(slot, chunk):
        move(part(right_ref, slot, chunk), part(right_ref, slot, chunk), 0, chunk, right_sem.at[slot, chunk], at(q, z, 1 - y, core)).wait_recv()

    def keep(ref, slot, which, chunk):
        return pltpu.make_async_copy(own_part(chunk), part(ref, slot, chunk), keep_sem.at[which, chunk])

    chunks = range(len(CHUNKS))
    for chunk in chunks:
        @pl.when(left_own)
        def _():
            keep(left_ref, near_slot(land), 0, chunk).start()

        @pl.when(jnp.logical_not(left_own))
        def _():
            left_skew(chunk).start()

        @pl.when(right_own)
        def _():
            keep(right_ref, own_slot(first), 1, chunk).start()

        @pl.when(jnp.logical_not(right_own))
        def _():
            right_skew(chunk).start()

    def crosses(index):
        return straight | (index == 1) & (shift == -1) | (index == 0) & (shift == 1)

    def shares(index):
        return index != 2 * core

    def landed(chunk):
        @pl.when(right_own)
        def _():
            keep(right_ref, own_slot(first), 1, chunk).wait()

        @pl.when(jnp.logical_not(right_own))
        def _():
            right_here(own_slot(first), chunk)

        right_send1(chunk).start()

        @pl.when(shares(first))
        def _():
            right_share(first, 8, chunk).start()

        @pl.when(left_own)
        def _():
            keep(left_ref, near_slot(land), 0, chunk).wait()

        @pl.when(jnp.logical_not(left_own))
        def _():
            left_here(near_slot(land), chunk)

        left_next(chunk).start()

        @pl.when(crosses(land))
        def _():
            left_cross(land, 2, chunk).start()

    def passed(chunk):
        right_here(own_slot(second), chunk)
        right_send2(chunk).start()

        @pl.when(shares(second))
        def _():
            right_share(second, 9, chunk).start()

        left_here(near_slot(1 - land), chunk)

        @pl.when(crosses(1 - land))
        def _():
            left_cross(1 - land, 3, chunk).start()

        left_here(cross_slot(core), chunk)

        @pl.when(passes)
        def _():
            left_pass(chunk).start()

    def ended(chunk):
        right_here(own_slot(third), chunk)

        @pl.when(shares(third))
        def _():
            right_share(third, 10, chunk).start()

        left_here(cross_slot(1 - core), chunk)

    for turn in range(len(CHUNKS) + 2):
        if turn < len(CHUNKS):
            landed(turn)
        if 1 <= turn <= len(CHUNKS):
            passed(turn - 1)
        if turn >= 2:
            ended(turn - 2)

    for chunk in chunks:
        for index in range(2):
            right_here(2 * (index + core) + 1 - 2 * core - y, chunk)

        @pl.when(jnp.logical_not(left_own))
        def _():
            left_skew(chunk).wait_send()

        left_next(chunk).wait_send()

        @pl.when(crosses(land))
        def _():
            left_cross(land, 2, chunk).wait_send()

        @pl.when(crosses(1 - land))
        def _():
            left_cross(1 - land, 3, chunk).wait_send()

        @pl.when(passes)
        def _():
            left_pass(chunk).wait_send()

        @pl.when(jnp.logical_not(right_own))
        def _():
            right_skew(chunk).wait_send()

        right_send1(chunk).wait_send()
        right_send2(chunk).wait_send()
        for index, kind in ((first, 8), (second, 9), (third, 10)):
            @pl.when(shares(index))
            def _():
                right_share(index, kind, chunk).wait_send()


def gather_tiles(data, cols):
    count = len(CHUNKS)
    return pl.pallas_call(
        gather_kernel,
        out_shape=(
            jax.ShapeDtypeStruct((4, ROWS, 256), jnp.float32),
            jax.ShapeDtypeStruct((5, ROWS, 256), jnp.float32),
        ),
        in_specs=[pl.BlockSpec(memory_space=pl.ANY)] * 2,
        out_specs=[pl.BlockSpec(memory_space=pl.ANY)] * 2,
        scratch_shapes=[
            pltpu.VMEM((ROWS, 256), jnp.float32),
            pltpu.SemaphoreType.DMA((2,)),
            pltpu.SemaphoreType.DMA((2, count)),
            pltpu.SemaphoreType.DMA((11, count)),
            pltpu.SemaphoreType.DMA((4, count)),
            pltpu.SemaphoreType.DMA((5, count)),
        ],
        compiler_params=pltpu.CompilerParams(collective_id=0, has_side_effects=True),
        name="gather_tiles",
    )(data, cols)


def product_kernel(left_cols, right_cols, left_ref, right_ref, out_ref, high, low):
    turn = pl.program_id(0)

    @pl.when(turn < STEPS)
    def _():
        side = lax.broadcasted_iota(jnp.int32, (BS, 128), 1) // BS

        def spread(inner, carry):
            block = right_ref[0, pl.ds(pl.multiple_of(inner * BS, BS), BS), :]
            top = block.astype(jnp.bfloat16)
            rest = (block - top.astype(jnp.float32)).astype(jnp.bfloat16)
            here = pl.ds(pl.multiple_of(inner * BS, BS), BS)
            targets = [right_cols[turn, inner * 4 + slot] for slot in range(4)]
            for value, kept in ((top, high), (rest, low)):
                doubled = []
                for pair in range(2):
                    both = value[:, pair * 128 : pair * 128 + 128]
                    even, uneven = both[:, :BS], both[:, BS:]
                    doubled.append(jnp.concatenate([even, even], axis=1))
                    doubled.append(jnp.concatenate([uneven, uneven], axis=1))
                for group in range(8):
                    spot = side + 2 * group
                    result = jnp.zeros((BS, 128), jnp.bfloat16)
                    for slot in range(4):
                        result = jnp.where(spot == targets[slot], doubled[slot], result)
                    kept[turn, here, group * 128 : group * 128 + 128] = result
            return carry

        lax.fori_loop(0, 16, spread, 0)

    @pl.when(turn >= STEPS)
    def _():
        block_row = turn - STEPS
        lane = lax.broadcasted_iota(jnp.int32, (BS, 256), 1) // BS
        tops, rests, starts = [], [], []
        for step in range(STEPS):
            used = jnp.zeros((BS, 256), jnp.bool_)
            for slot in range(4):
                inner = left_cols[step, block_row * 4 + slot]
                used = used | (lane == jnp.where(inner >= 0, slot, -1))
                starts.append((step, pl.multiple_of(jnp.maximum(inner, 0) * BS, BS)))
            block = jnp.where(used, left_ref[step], 0.0)
            top = block.astype(jnp.bfloat16)
            tops.append(top)
            rests.append((block - top.astype(jnp.float32)).astype(jnp.bfloat16))
        top = jnp.concatenate(tops, axis=1)
        both = jnp.concatenate([top, jnp.concatenate(rests, axis=1)], axis=0)
        for quarter in range(4):
            lanes = slice(quarter * 256, quarter * 256 + 256)
            right_top = jnp.concatenate([high[step, pl.ds(start, BS), lanes] for step, start in starts], axis=0)
            right_rest = jnp.concatenate([low[step, pl.ds(start, BS), lanes] for step, start in starts], axis=0)
            main = jnp.dot(both, right_top, preferred_element_type=jnp.float32)
            extra = jnp.dot(top, right_rest, preferred_element_type=jnp.float32)
            out_ref[:, lanes] = main[:BS] + main[BS:] + extra


def multiply(left_cols, right_cols, left, right):
    return pl.pallas_call(
        product_kernel,
        out_shape=jax.ShapeDtypeStruct((1024, 1024), jnp.float32),
        grid_spec=pltpu.PrefetchScalarGridSpec(
            num_scalar_prefetch=2,
            grid=(STEPS + 16,),
            in_specs=[
                pl.BlockSpec((4, BS, 256), lambda turn, *_: (0, jnp.maximum(turn - STEPS, 0), 0)),
                pl.BlockSpec((1, 1024, 256), lambda turn, *_: (jnp.minimum(turn, STEPS - 1), 0, 0)),
            ],
            out_specs=pl.BlockSpec((BS, 1024), lambda turn, *_: (jnp.maximum(turn - STEPS, 0), 0)),
            scratch_shapes=[
                pltpu.VMEM((STEPS, 1024, 1024), jnp.bfloat16),
                pltpu.VMEM((STEPS, 1024, 1024), jnp.bfloat16),
            ],
        ),
        name="multiply",
    )(left_cols, right_cols, left, right)


def local(p_cols, p_data):
    cols = jnp.pad(p_cols.astype(jnp.float32).reshape(1, 64), ((0, 7), (0, 192)))
    left, right = gather_tiles(p_data, cols)
    left_cols = left[:, 1024, :64].astype(jnp.int32)
    right_cols = right[:4, 1024, :64].astype(jnp.int32)
    return multiply(left_cols, right_cols, left, right)


def solution(mesh):
    return jax.shard_map(
        local, mesh=mesh, in_specs=(P("row", "col"), P("row", "col")), out_specs=P("row", "col"), check_vma=False
    )
```

```python
import functools

import jax
import jax.numpy as jnp
from jax import lax
from jax.experimental import pallas as pl
from jax.experimental.pallas import tpu as pltpu
from jax.sharding import PartitionSpec as P

BS = 64
STEPS = 4
PIECES = 4
PIECE_ROWS = 1024 // PIECES
PIECE_BLOCKS = PIECE_ROWS // BS
COLS = PIECES
ALL = (COLS,) + tuple(range(PIECES))
MESH = pl.DeviceIdType.MESH


def kernel(
    cols_hbm, data_hbm, out_hbm,
    own, own_cols, left, left_cols, right, right_cols, high, low, out, left_at, right_at,
    load_sem, keep_sem, send_sem, left_sem, right_sem, at_sem, out_sem,
):
    row, col = lax.axis_index("row"), lax.axis_index("col")
    q, core = row // 2, row % 2
    half = q % 2
    z, y = col // 2, col % 2
    odd = z % 2 == 1

    def at(q_new, z_new, y_new, core_new):
        return (2 * ((q_new + 32) % 8) + core_new, 2 * ((z_new + 32) % 8) + y_new)

    depth = q + core
    land = jnp.where((depth >= 5) & (depth <= 7) | (depth >= 3) & (depth <= 4) & (core == 1), 1, 0)
    skew = depth + land
    left_own = skew % 8 == 0
    lane = 2 * land - 1

    def near_slot(index):
        return 2 * index + core

    def cross_slot(index):
        return 2 * index + 1 - core

    def cross_at(y_here):
        free = jnp.where(q <= 2, 1, jnp.where(q >= 4, 0, core))
        return jnp.where(y_here == core, free, core)

    crossed = cross_at(y)
    pass_lane = 2 * crossed - 1
    cross_as = cross_at(1 - y)
    cross_of = 1 - y + cross_as - core

    first = jnp.where(odd, 1, jnp.where(z < 4, 0, 2))
    right_own = (z + first) % 8 == 0
    second = jnp.where(odd, 2 - 2 * half, 2 - first)
    third = 3 - first - second

    def own_slot(index):
        return (2 * index - y + 5) % 5

    def shared_slot(index):
        return 2 * (index + core) + 1 - 2 * core - y

    hop = 1 - 2 * half
    send1_to = q + jnp.where(odd, hop, 2 * first - 2)
    send1_as = jnp.where(odd, 1 - hop, 2 - first)
    send2_of = jnp.where(odd, second, 2 - 2 * half)
    send2_to = q + jnp.where(odd, 2 * hop, hop)
    send2_as = jnp.where(odd, third, 1)

    barrier = pltpu.get_barrier_semaphore()

    def greet(device):
        pl.semaphore_signal(barrier, inc=1, device_id=device, device_id_type=MESH)

    @pl.when(jnp.logical_not(left_own))
    def _():
        greet(at(q, z + skew, y, core))

    greet(at(q, z - lane, y, core))
    greet(at(q, z, 1 - y, core))
    greet(at(q, z - pass_lane, y, core))

    @pl.when(jnp.logical_not(right_own))
    def _():
        greet(at(q + z + first, z, y, core))

    greet(at(q + jnp.where(odd, hop, 2 - 2 * first), z, y, core))
    greet(at(q + jnp.where(odd, -2 * hop, hop), z, y, core))
    greet(at(q, z, y, 1 - core))

    load = pltpu.make_async_copy(data_hbm, own, load_sem.at[0])
    load_cols = pltpu.make_async_copy(cols_hbm, own_cols, load_sem.at[1])
    load.start()
    load_cols.start()
    load.wait()
    load_cols.wait()
    pl.semaphore_wait(barrier, 8 - left_own.astype(jnp.int32) - right_own.astype(jnp.int32))

    def rows(piece):
        return pl.ds(piece * PIECE_ROWS, PIECE_ROWS)

    def own_part(piece):
        return own_cols if piece == COLS else own.at[rows(piece)]

    def left_part(slot, piece):
        return left_cols.at[slot] if piece == COLS else left.at[slot, rows(piece)]

    def right_part(slot, piece):
        return right_cols.at[slot] if piece == COLS else right.at[slot, rows(piece)]

    def move(source, target, kind, piece, sem, device):
        return pltpu.make_async_remote_copy(
            src_ref=source,
            dst_ref=target,
            send_sem=send_sem.at[kind, piece],
            recv_sem=sem,
            device_id=device,
            device_id_type=MESH,
        )

    def to_left(source, slot, kind, piece, device):
        return move(source, left_part(slot, piece), kind, piece, left_sem.at[slot, piece], device)

    def to_right(source, slot, kind, piece, device):
        return move(source, right_part(slot, piece), kind, piece, right_sem.at[slot, piece], device)

    def left_skew(piece):
        return to_left(own_part(piece), near_slot(land), 0, piece, at(q, z - skew, y, core))

    def left_next(piece):
        return to_left(left_part(near_slot(land), piece), near_slot(1 - land), 1, piece, at(q, z + lane, y, core))

    def left_cross(piece):
        return to_left(left_part(near_slot(cross_of), piece), cross_slot(cross_as), 2, piece, at(q, z, 1 - y, core))

    def left_pass(piece):
        source = left_part(cross_slot(crossed), piece)
        return to_left(source, cross_slot(1 - crossed), 3, piece, at(q, z + pass_lane, y, core))

    def right_skew(piece):
        return to_right(own_part(piece), own_slot(first), 4, piece, at(q - z - first, z, y, core))

    def right_send1(piece):
        return to_right(right_part(own_slot(first), piece), own_slot(send1_as), 5, piece, at(send1_to, z, y, core))

    def right_send2(piece):
        return to_right(right_part(own_slot(send2_of), piece), own_slot(send2_as), 6, piece, at(send2_to, z, y, core))

    def right_share(index, kind, piece):
        slot = 2 * index - 1 + 2 * core - y
        return to_right(right_part(own_slot(index), piece), slot, kind, piece, at(q, z, y, 1 - core))

    def left_here(slot, piece):
        to_left(left_part(slot, piece), slot, 0, piece, at(q, z, 1 - y, core)).wait_recv()

    def right_here(slot, piece):
        to_right(right_part(slot, piece), slot, 0, piece, at(q, z, 1 - y, core)).wait_recv()

    def keep_left(piece):
        return pltpu.make_async_copy(own_part(piece), left_part(near_slot(land), piece), keep_sem.at[0, piece])

    def keep_right(piece):
        return pltpu.make_async_copy(own_part(piece), right_part(own_slot(first), piece), keep_sem.at[1, piece])

    def shares(index):
        return index != 2 * core

    side = lax.broadcasted_iota(jnp.int32, (BS, 128), 1) // BS

    def spread(slot, piece):
        def one(index, carry):
            inner = piece * PIECE_BLOCKS + index
            here = pl.ds(pl.multiple_of(inner * BS, BS), BS)
            block = right[slot, here, :]
            top = block.astype(jnp.bfloat16)
            rest = (block - top.astype(jnp.float32)).astype(jnp.bfloat16)
            targets = [right_at[slot, inner, place] for place in range(4)]
            for value, kept in ((top, high), (rest, low)):
                doubled = []
                for pair in range(2):
                    both = value[:, pair * 128 : pair * 128 + 128]
                    even, uneven = both[:, :BS], both[:, BS:]
                    doubled.append(jnp.concatenate([even, even], axis=1))
                    doubled.append(jnp.concatenate([uneven, uneven], axis=1))
                for group in range(8):
                    spot = side + 2 * group
                    result = jnp.zeros((BS, 128), jnp.bfloat16)
                    for place in range(4):
                        result = jnp.where(spot == targets[place], doubled[place], result)
                    kept[slot, inner, :, group * 128 : group * 128 + 128] = result
            return carry

        lax.fori_loop(0, PIECE_BLOCKS, one, 0)

    def right_ready(slot, piece):
        if piece == COLS:
            copy = pltpu.make_async_copy(right_cols.at[slot], right_at.at[slot], at_sem)
            copy.start()
            copy.wait()
        else:
            spread(slot, piece)

    def own_ready(index, piece):
        @pl.when(own_slot(index) < 4)
        def _():
            right_ready(own_slot(index), piece)

    def products(piece):
        def one(index, carry):
            block_row = piece * PIECE_BLOCKS + index
            here = pl.ds(pl.multiple_of(block_row * BS, BS), BS)
            place = lax.broadcasted_iota(jnp.int32, (BS, 256), 1) // BS
            tops, rests, starts = [], [], []
            for step in range(STEPS):
                used = jnp.zeros((BS, 256), jnp.bool_)
                for slot in range(4):
                    inner = left_at[step, block_row, slot]
                    used = used | (place == jnp.where(inner >= 0, slot, -1))
                    starts.append((step, jnp.maximum(inner, 0)))
                block = jnp.where(used, left[step, here, :], 0.0)
                top = block.astype(jnp.bfloat16)
                tops.append(top)
                rests.append((block - top.astype(jnp.float32)).astype(jnp.bfloat16))
            top = jnp.concatenate(tops, axis=1)
            both = jnp.concatenate([top, jnp.concatenate(rests, axis=1)], axis=0)
            for quarter in range(4):
                lanes = slice(quarter * 256, quarter * 256 + 256)
                right_top = jnp.concatenate([high[step, start, :, lanes] for step, start in starts], axis=0)
                right_rest = jnp.concatenate([low[step, start, :, lanes] for step, start in starts], axis=0)
                main = jnp.dot(both, right_top, preferred_element_type=jnp.float32)
                extra = jnp.dot(top, right_rest, preferred_element_type=jnp.float32)
                out[here, lanes] = main[:BS] + main[BS:] + extra
            return carry

        lax.fori_loop(0, PIECE_BLOCKS, one, 0)
        write(piece).start()

    def write(piece):
        return pltpu.make_async_copy(out.at[rows(piece)], out_hbm.at[rows(piece)], out_sem.at[piece])

    for piece in ALL:
        @pl.when(left_own)
        def _():
            keep_left(piece).start()

        @pl.when(jnp.logical_not(left_own))
        def _():
            left_skew(piece).start()

        @pl.when(right_own)
        def _():
            keep_right(piece).start()

        @pl.when(jnp.logical_not(right_own))
        def _():
            right_skew(piece).start()

    def right_first(piece):
        @pl.when(right_own)
        def _():
            keep_right(piece).wait()

        @pl.when(jnp.logical_not(right_own))
        def _():
            right_here(own_slot(first), piece)

        right_send1(piece).start()

        @pl.when(shares(first))
        def _():
            right_share(first, 7, piece).start()

    def right_second(piece):
        right_here(own_slot(second), piece)
        right_send2(piece).start()

        @pl.when(shares(second))
        def _():
            right_share(second, 8, piece).start()

    def right_third(piece):
        right_here(own_slot(third), piece)

        @pl.when(shares(third))
        def _():
            right_share(third, 9, piece).start()

    def left_first(piece):
        @pl.when(left_own)
        def _():
            keep_left(piece).wait()

        @pl.when(jnp.logical_not(left_own))
        def _():
            left_here(near_slot(land), piece)

        left_next(piece).start()

        @pl.when(cross_of == land)
        def _():
            left_cross(piece).start()

    def left_second(piece):
        left_here(near_slot(1 - land), piece)

        @pl.when(cross_of != land)
        def _():
            left_cross(piece).start()

    def left_third(piece):
        left_here(cross_slot(crossed), piece)
        left_pass(piece).start()

    def left_last(piece):
        left_here(cross_slot(1 - crossed), piece)

    def lagged(stages):
        for turn in range(len(ALL) + len(stages) - 1):
            for lag, stage in enumerate(stages):
                if 0 <= turn - lag < len(ALL):
                    stage(ALL[turn - lag])

    def landed(piece):
        right_first(piece)
        left_first(piece)
        own_ready(first, piece)

    def followed(piece):
        right_second(piece)
        own_ready(second, piece)

    def finished(piece):
        right_third(piece)
        left_second(piece)
        own_ready(third, piece)

    def shared(piece):
        left_third(piece)
        for index in range(2):
            right_here(shared_slot(index), piece)
            right_ready(shared_slot(index), piece)

    lagged((landed, followed))
    lagged((finished, shared))
    for piece in ALL:
        left_last(piece)
        if piece == COLS:
            copy = pltpu.make_async_copy(left_cols, left_at, at_sem)
            copy.start()
            copy.wait()
        else:
            products(piece)

    for piece in ALL:
        @pl.when(jnp.logical_not(left_own))
        def _():
            left_skew(piece).wait_send()

        @pl.when(jnp.logical_not(right_own))
        def _():
            right_skew(piece).wait_send()

        left_next(piece).wait_send()
        left_cross(piece).wait_send()
        left_pass(piece).wait_send()
        right_send1(piece).wait_send()
        right_send2(piece).wait_send()
        for index, kind in ((first, 7), (second, 8), (third, 9)):
            @pl.when(shares(index))
            def _():
                right_share(index, kind, piece).wait_send()

        if piece != COLS:
            write(piece).wait()


def local(p_cols, p_data):
    count = len(ALL)
    return pl.pallas_call(
        kernel,
        out_shape=jax.ShapeDtypeStruct((1024, 1024), jnp.float32),
        in_specs=[pl.BlockSpec(memory_space=pl.ANY)] * 2,
        out_specs=pl.BlockSpec(memory_space=pl.ANY),
        scratch_shapes=[
            pltpu.VMEM((1024, 256), jnp.float32),
            pltpu.VMEM((16, 4), jnp.int32),
            pltpu.VMEM((4, 1024, 256), jnp.float32),
            pltpu.VMEM((4, 16, 4), jnp.int32),
            pltpu.VMEM((5, 1024, 256), jnp.float32),
            pltpu.VMEM((5, 16, 4), jnp.int32),
            pltpu.VMEM((STEPS, 16, BS, 1024), jnp.bfloat16),
            pltpu.VMEM((STEPS, 16, BS, 1024), jnp.bfloat16),
            pltpu.VMEM((1024, 1024), jnp.float32),
            pltpu.SMEM((4, 16, 4), jnp.int32),
            pltpu.SMEM((4, 16, 4), jnp.int32),
            pltpu.SemaphoreType.DMA((2,)),
            pltpu.SemaphoreType.DMA((2, count)),
            pltpu.SemaphoreType.DMA((10, count)),
            pltpu.SemaphoreType.DMA((4, count)),
            pltpu.SemaphoreType.DMA((5, count)),
            pltpu.SemaphoreType.DMA,
            pltpu.SemaphoreType.DMA((PIECES,)),
        ],
        compiler_params=pltpu.CompilerParams(collective_id=0, has_side_effects=True),
        name="window_square",
    )(p_cols, p_data)


def solution(mesh):
    return jax.shard_map(
        local, mesh=mesh, in_specs=(P("row", "col"), P("row", "col")), out_specs=P("row", "col"), check_vma=False
    )
```

```python
import functools

import jax
import jax.numpy as jnp
from jax import lax
from jax.experimental import pallas as pl
from jax.experimental.pallas import tpu as pltpu
from jax.sharding import PartitionSpec as P

BS = 64
STEPS = 4
PIECES = 8
PIECE_ROWS = 1024 // PIECES
PIECE_BLOCKS = PIECE_ROWS // BS
COLS = PIECES
LEFT_AHEAD = 3
RIGHT_AHEAD = 3
RIGHT_PACE = 0.6
RIGHT_LAG = 1.4
LEFT_LAG = 2.0
END_LAG = 2.0
ALL = (COLS,) + tuple(range(PIECES))
MESH = pl.DeviceIdType.MESH


def kernel(
    cols_hbm, data_hbm, out_hbm,
    own, own_cols, left, left_cols, right, right_cols, relay, high, low, out, left_at, right_at,
    load_sem, keep_sem, send_sem, left_sem, right_sem, relay_sem, at_sem, out_sem,
):
    row, col = lax.axis_index("row"), lax.axis_index("col")
    q, core = row // 2, row % 2
    half = q % 2
    z, y = col // 2, col % 2
    odd = z % 2 == 1

    def at(q_new, z_new, y_new, core_new):
        return (2 * ((q_new + 32) % 8) + core_new, 2 * ((z_new + 32) % 8) + y_new)

    depth = q + core
    land = jnp.where((depth >= 5) & (depth <= 7) | (q == 3) & (core == 1) | (q == 4) & (core == 0), 1, 0)
    skew = depth + land
    left_own = skew % 8 == 0
    lane = 2 * land - 1
    some = (q == 1) & (core == 1) | (q == 5) & (core == 0)
    most = (q == 2) & (core == 1) | (q == 4) & (core == 0)
    relays = some | most
    long_lane = -lane
    long_way = jnp.where(land == 0, 7 - depth, depth)

    def takes_long(piece):
        if piece == COLS or piece % 4 == 3:
            return q < 0
        return relays if piece % 4 == 0 else most

    def land_of(piece):
        return jnp.where(takes_long(piece), 1 - land, land)

    def lane_of(piece):
        return jnp.where(takes_long(piece), long_lane, lane)

    def near_slot(index):
        return 2 * index + core

    def cross_slot(index):
        return 2 * index + 1 - core

    def cross_at(y_here):
        free = jnp.where(q <= 1, 1, jnp.where(q >= 5, 0, core))
        return jnp.where(y_here == core, free, core)

    crossed = cross_at(y)
    pass_lane = 2 * crossed - 1
    cross_as = cross_at(1 - y)
    cross_of = 1 - y + cross_as - core

    first = jnp.where(odd, 1, jnp.where(z == 0, 0, jnp.where(z == 6, 2, 2 * core)))
    right_own = (z + first) % 8 == 0
    second = jnp.where(odd, 2 - 2 * half, 2 - first)
    third = 3 - first - second

    def own_slot(index):
        return (2 * index - y + 5) % 5

    def shared_slot(index):
        return 2 * (index + core) + 1 - 2 * core - y

    hop = 1 - 2 * half
    send1_to = q + jnp.where(odd, hop, 2 * first - 2)
    send1_as = jnp.where(odd, 1 - hop, 2 - first)
    send2_of = jnp.where(odd, second, 2 - 2 * half)
    send2_to = q + jnp.where(odd, 2 * hop, hop)
    send2_as = jnp.where(odd, third, 1)

    barrier = pltpu.get_barrier_semaphore()

    def greet(device):
        pl.semaphore_signal(barrier, inc=1, device_id=device, device_id_type=MESH)

    @pl.when(jnp.logical_not(left_own))
    def _():
        greet(at(q, z + skew, y, core))

    greet(at(q, z - lane, y, core))

    @pl.when(relays)
    def _():
        greet(at(q, z - long_lane, y, core))
        greet(at(q, z - long_lane * (long_way - 2), y, core))
        greet(at(q, z - long_lane * 2, y, core))

    greet(at(q, z, 1 - y, core))
    greet(at(q, z - pass_lane, y, core))

    @pl.when(jnp.logical_not(right_own))
    def _():
        greet(at(q + z + first, z, y, core))

    greet(at(q + jnp.where(odd, hop, 2 - 2 * first), z, y, core))
    greet(at(q + jnp.where(odd, -2 * hop, hop), z, y, core))
    greet(at(q, z, y, 1 - core))

    load = pltpu.make_async_copy(data_hbm, own, load_sem.at[0])
    load_cols = pltpu.make_async_copy(cols_hbm, own_cols, load_sem.at[1])
    load.start()
    load_cols.start()
    load.wait()
    load_cols.wait()
    absent = left_own.astype(jnp.int32) + right_own.astype(jnp.int32)
    pl.semaphore_wait(barrier, 8 - absent + jnp.where(relays, 3, 0))

    def rows(piece):
        return pl.ds(piece * PIECE_ROWS, PIECE_ROWS)

    def own_part(piece):
        return own_cols if piece == COLS else own.at[rows(piece)]

    def left_part(slot, piece):
        return left_cols.at[slot] if piece == COLS else left.at[slot, rows(piece)]

    def right_part(slot, piece):
        return right_cols.at[slot] if piece == COLS else right.at[slot, rows(piece)]

    def move(source, target, kind, piece, sem, device):
        return pltpu.make_async_remote_copy(
            src_ref=source,
            dst_ref=target,
            send_sem=send_sem.at[kind, piece],
            recv_sem=sem,
            device_id=device,
            device_id_type=MESH,
        )

    def to_left(source, slot, kind, piece, device):
        return move(source, left_part(slot, piece), kind, piece, left_sem.at[slot, piece], device)

    def to_right(source, slot, kind, piece, device):
        return move(source, right_part(slot, piece), kind, piece, right_sem.at[slot, piece], device)

    def left_skew(piece):
        return to_left(own_part(piece), near_slot(land), 0, piece, at(q, z - skew, y, core))

    def left_long(piece):
        device = at(q, z + long_lane * (long_way - 2), y, core)
        return move(own_part(piece), relay.at[piece], 0, piece, relay_sem.at[piece], device)

    def left_relay(piece):
        return to_left(relay.at[piece], near_slot(1 - land), 10, piece, at(q, z + long_lane * 2, y, core))

    def left_next(piece):
        here, there = near_slot(land_of(piece)), near_slot(1 - land_of(piece))
        return to_left(left_part(here, piece), there, 1, piece, at(q, z + lane_of(piece), y, core))

    def left_cross(piece):
        return to_left(left_part(near_slot(cross_of), piece), cross_slot(cross_as), 2, piece, at(q, z, 1 - y, core))

    def left_pass(piece):
        source = left_part(cross_slot(crossed), piece)
        return to_left(source, cross_slot(1 - crossed), 3, piece, at(q, z + pass_lane, y, core))

    def right_skew(piece):
        return to_right(own_part(piece), own_slot(first), 4, piece, at(q - z - first, z, y, core))

    def right_send1(piece):
        return to_right(right_part(own_slot(first), piece), own_slot(send1_as), 5, piece, at(send1_to, z, y, core))

    def right_send2(piece):
        return to_right(right_part(own_slot(send2_of), piece), own_slot(send2_as), 6, piece, at(send2_to, z, y, core))

    def right_share(index, kind, piece):
        slot = 2 * index - 1 + 2 * core - y
        return to_right(right_part(own_slot(index), piece), slot, kind, piece, at(q, z, y, 1 - core))

    def left_here(slot, piece):
        to_left(left_part(slot, piece), slot, 0, piece, at(q, z, 1 - y, core)).wait_recv()

    def right_here(slot, piece):
        to_right(right_part(slot, piece), slot, 0, piece, at(q, z, 1 - y, core)).wait_recv()

    def keep_left(piece):
        return pltpu.make_async_copy(own_part(piece), left_part(near_slot(land), piece), keep_sem.at[0, piece])

    def keep_right(piece):
        return pltpu.make_async_copy(own_part(piece), right_part(own_slot(first), piece), keep_sem.at[1, piece])

    def shares(index):
        return index != 2 * core

    side = lax.broadcasted_iota(jnp.int32, (BS, 128), 1) // BS

    def spread(slot, piece):
        def one(index, carry):
            inner = piece * PIECE_BLOCKS + index
            here = pl.ds(pl.multiple_of(inner * BS, BS), BS)
            block = right[slot, here, :]
            top = block.astype(jnp.bfloat16)
            rest = (block - top.astype(jnp.float32)).astype(jnp.bfloat16)
            targets = [right_at[slot, place, inner] for place in range(4)]
            for value, kept in ((top, high), (rest, low)):
                doubled = []
                for pair in range(2):
                    both = value[:, pair * 128 : pair * 128 + 128]
                    even, uneven = both[:, :BS], both[:, BS:]
                    doubled.append(jnp.concatenate([even, even], axis=1))
                    doubled.append(jnp.concatenate([uneven, uneven], axis=1))
                for group in range(8):
                    spot = side + 2 * group
                    result = jnp.zeros((BS, 128), jnp.bfloat16)
                    for place in range(4):
                        result = jnp.where(spot == targets[place], doubled[place], result)
                    kept[slot, inner, :, group * 128 : group * 128 + 128] = result
            return carry

        lax.fori_loop(0, PIECE_BLOCKS, one, 0)

    def right_ready(slot, piece):
        if piece == COLS:
            copy = pltpu.make_async_copy(right_cols.at[slot], right_at.at[slot], at_sem)
            copy.start()
            copy.wait()
        else:
            spread(slot, piece)

    def own_ready(index, piece):
        @pl.when(own_slot(index) < 4)
        def _():
            right_ready(own_slot(index), piece)

    def products(piece, slots, fresh):
        def one(index, carry):
            block_row = piece * PIECE_BLOCKS + index
            here = pl.ds(pl.multiple_of(block_row * BS, BS), BS)
            place = lax.broadcasted_iota(jnp.int32, (BS, 256), 1) // BS
            tops, rests, starts = [], [], []
            for step in slots:
                used = jnp.zeros((BS, 256), jnp.bool_)
                for slot in range(4):
                    inner = left_at[step, slot, block_row]
                    used = used | (place == jnp.where(inner >= 0, slot, -1))
                    starts.append((step, jnp.maximum(inner, 0)))
                block = jnp.where(used, left[step, here, :], 0.0)
                top = block.astype(jnp.bfloat16)
                tops.append(top)
                rests.append((block - top.astype(jnp.float32)).astype(jnp.bfloat16))
            top = jnp.concatenate(tops, axis=1)
            both = jnp.concatenate([top, jnp.concatenate(rests, axis=1)], axis=0)
            for quarter in range(4):
                lanes = slice(quarter * 256, quarter * 256 + 256)
                right_top = jnp.concatenate([high[step, start, :, lanes] for step, start in starts], axis=0)
                right_rest = jnp.concatenate([low[step, start, :, lanes] for step, start in starts], axis=0)
                main = jnp.dot(both, right_top, preferred_element_type=jnp.float32)
                extra = jnp.dot(top, right_rest, preferred_element_type=jnp.float32)
                term = main[:BS] + main[BS:] + extra
                out[here, lanes] = term if fresh else out[here, lanes] + term
            return carry

        lax.fori_loop(0, PIECE_BLOCKS, one, 0)

    def write(piece):
        return pltpu.make_async_copy(out.at[rows(piece)], out_hbm.at[rows(piece)], out_sem.at[piece])

    def left_start(piece):
        @pl.when(left_own)
        def _():
            keep_left(piece).start()

        @pl.when(jnp.logical_not(left_own | takes_long(piece)))
        def _():
            left_skew(piece).start()

        if piece != COLS:
            @pl.when(takes_long(piece))
            def _():
                left_long(piece).start()

    def right_start(piece):
        @pl.when(right_own)
        def _():
            keep_right(piece).start()

        @pl.when(jnp.logical_not(right_own))
        def _():
            right_skew(piece).start()

    def start_after(start, piece, ahead):
        place = ALL.index(piece) + ahead
        if place < len(ALL):
            start(ALL[place])

    for piece in ALL[:RIGHT_AHEAD]:
        right_start(piece)
    for piece in ALL[:LEFT_AHEAD]:
        left_start(piece)

    def right_first(piece):
        @pl.when(right_own)
        def _():
            keep_right(piece).wait()

        @pl.when(jnp.logical_not(right_own))
        def _():
            right_here(own_slot(first), piece)

        right_send1(piece).start()

        @pl.when(shares(first))
        def _():
            right_share(first, 7, piece).start()

    def right_second(piece):
        right_here(own_slot(second), piece)
        right_send2(piece).start()

        @pl.when(shares(second))
        def _():
            right_share(second, 8, piece).start()

    def right_third(piece):
        right_here(own_slot(third), piece)

        @pl.when(shares(third))
        def _():
            right_share(third, 9, piece).start()

    def left_first(piece):
        @pl.when(left_own)
        def _():
            keep_left(piece).wait()

        @pl.when(jnp.logical_not(left_own))
        def _():
            left_here(near_slot(land_of(piece)), piece)

        left_next(piece).start()

        @pl.when(cross_of == land_of(piece))
        def _():
            left_cross(piece).start()

    def left_second(piece):
        left_here(near_slot(1 - land_of(piece)), piece)

        @pl.when(cross_of != land_of(piece))
        def _():
            left_cross(piece).start()

    def left_third(piece):
        left_here(cross_slot(crossed), piece)
        left_pass(piece).start()

    def left_last(piece):
        left_here(cross_slot(1 - crossed), piece)

    def relayed(piece):
        if piece != COLS:
            @pl.when(takes_long(piece))
            def _():
                move(relay.at[piece], relay.at[piece], 0, piece, relay_sem.at[piece], at(q, z, 1 - y, core)).wait_recv()
                left_relay(piece).start()

    def right_landed(piece):
        right_first(piece)
        start_after(right_start, piece, RIGHT_AHEAD)
        own_ready(first, piece)

    def right_followed(piece):
        right_second(piece)
        own_ready(second, piece)

    def right_finished(piece):
        right_third(piece)
        own_ready(third, piece)

    def right_shared(piece):
        for index in range(2):
            right_here(shared_slot(index), piece)
            right_ready(shared_slot(index), piece)

    def left_landed(piece):
        left_first(piece)
        start_after(left_start, piece, LEFT_AHEAD)

    def left_ended(piece):
        left_last(piece)
        if piece == COLS:
            copy = pltpu.make_async_copy(left_cols, left_at, at_sem)
            copy.start()
            copy.wait()

    def near_products(piece):
        products(piece, (near_slot(0), near_slot(1)), True)

    def crossed_products(piece):
        products(piece, (cross_slot(crossed),), False)

    def last_products(piece):
        products(piece, (cross_slot(1 - crossed),), False)
        write(piece).start()

    events = []
    for place, piece in enumerate(ALL):
        right_turn, left_turn = place * RIGHT_PACE, place + 0.3
        for lag, stage in enumerate((right_landed, right_followed, right_finished, right_shared)):
            events.append((right_turn + lag * RIGHT_LAG, stage, piece))
        for lag, stage in enumerate((relayed, left_landed, left_second, left_third)):
            events.append((left_turn + (lag - 0.5) * LEFT_LAG, stage, piece))
        events.append((left_turn + 2.5 * LEFT_LAG + END_LAG, left_ended, piece))
    ready = max(turn for turn, stage, piece in events if stage is right_shared)
    at_turn = {(stage, piece): turn for turn, stage, piece in events}
    cols_turn = at_turn[left_ended, COLS]
    for place, piece in enumerate(ALL[1:]):
        least = max(ready, cols_turn) + 0.01 + 0.1 * place
        events.append((max(least, at_turn[left_second, piece] + 0.01), near_products, piece))
        events.append((max(least + 0.05, at_turn[left_third, piece] + 0.02), crossed_products, piece))
        events.append((max(least + 0.1, at_turn[left_ended, piece] + 0.01), last_products, piece))
    for turn, stage, piece in sorted(events, key=lambda event: event[0]):
        stage(piece)

    for piece in ALL:
        @pl.when(jnp.logical_not(left_own))
        def _():
            left_skew(piece).wait_send()

        @pl.when(jnp.logical_not(right_own))
        def _():
            right_skew(piece).wait_send()

        if piece != COLS:
            @pl.when(takes_long(piece))
            def _():
                left_relay(piece).wait_send()

        left_next(piece).wait_send()
        left_cross(piece).wait_send()
        left_pass(piece).wait_send()
        right_send1(piece).wait_send()
        right_send2(piece).wait_send()
        for index, kind in ((first, 7), (second, 8), (third, 9)):
            @pl.when(shares(index))
            def _():
                right_share(index, kind, piece).wait_send()

        if piece != COLS:
            write(piece).wait()


def local(p_cols, p_data):
    count = len(ALL)
    return pl.pallas_call(
        kernel,
        out_shape=jax.ShapeDtypeStruct((1024, 1024), jnp.float32),
        in_specs=[pl.BlockSpec(memory_space=pl.ANY)] * 2,
        out_specs=pl.BlockSpec(memory_space=pl.ANY),
        scratch_shapes=[
            pltpu.VMEM((1024, 256), jnp.float32),
            pltpu.VMEM((4, 16), jnp.int32),
            pltpu.VMEM((4, 1024, 256), jnp.float32),
            pltpu.VMEM((4, 4, 16), jnp.int32),
            pltpu.VMEM((5, 1024, 256), jnp.float32),
            pltpu.VMEM((5, 4, 16), jnp.int32),
            pltpu.VMEM((PIECES, PIECE_ROWS, 256), jnp.float32),
            pltpu.VMEM((STEPS, 16, BS, 1024), jnp.bfloat16),
            pltpu.VMEM((STEPS, 16, BS, 1024), jnp.bfloat16),
            pltpu.VMEM((1024, 1024), jnp.float32),
            pltpu.SMEM((4, 4, 16), jnp.int32),
            pltpu.SMEM((4, 4, 16), jnp.int32),
            pltpu.SemaphoreType.DMA((2,)),
            pltpu.SemaphoreType.DMA((2, count)),
            pltpu.SemaphoreType.DMA((11, count)),
            pltpu.SemaphoreType.DMA((4, count)),
            pltpu.SemaphoreType.DMA((5, count)),
            pltpu.SemaphoreType.DMA((PIECES,)),
            pltpu.SemaphoreType.DMA,
            pltpu.SemaphoreType.DMA((PIECES,)),
        ],
        compiler_params=pltpu.CompilerParams(collective_id=0, has_side_effects=True),
        name="window_square",
    )(p_cols.T, p_data)


def solution(mesh):
    return jax.shard_map(
        local, mesh=mesh, in_specs=(P("row", "col"), P("row", "col")), out_specs=P("row", "col"), check_vma=False
    )
```

```python
import functools

import jax
import jax.numpy as jnp
from jax import lax
from jax.experimental import pallas as pl
from jax.experimental.pallas import tpu as pltpu
from jax.sharding import PartitionSpec as P

BS = 64
STEPS = 4
PIECES = 8
PIECE_ROWS = 1024 // PIECES
PIECE_BLOCKS = PIECE_ROWS // BS
COLS = PIECES
LEFT_AHEAD = 3
RIGHT_AHEAD = 3
RIGHT_PACE = 0.6
RIGHT_LAG = 1.4
LEFT_LAG = 2.0
END_LAG = 2.0
SPACING = 0.1
ALL = (COLS,) + tuple(range(PIECES))
MESH = pl.DeviceIdType.MESH


def kernel(
    cols_hbm, data_hbm, out_hbm,
    left, left_cols, right, right_cols, relay, high, low, out, left_at, right_at,
    keep_sem, send_sem, left_sem, right_sem, relay_sem, at_sem, out_sem,
):
    row, col = lax.axis_index("row"), lax.axis_index("col")
    q, core = row // 2, row % 2
    half = q % 2
    z, y = col // 2, col % 2
    odd = z % 2 == 1

    def at(q_new, z_new, y_new, core_new):
        return (2 * ((q_new + 32) % 8) + core_new, 2 * ((z_new + 32) % 8) + y_new)

    depth = q + core
    land = jnp.where((depth >= 5) & (depth <= 7) | (q == 3) & (core == 1) | (q == 4) & (core == 0), 1, 0)
    skew = depth + land
    left_own = skew % 8 == 0
    lane = 2 * land - 1
    some = (q == 1) & (core == 1) | (q == 5) & (core == 0)
    most = (q == 2) & (core == 1) | (q == 4) & (core == 0)
    relays = some | most
    long_lane = -lane
    long_way = jnp.where(land == 0, 7 - depth, depth)

    def takes_long(piece):
        if piece == COLS or piece % 4 == 3:
            return q < 0
        return relays if piece % 4 == 0 else most

    def land_of(piece):
        return jnp.where(takes_long(piece), 1 - land, land)

    def lane_of(piece):
        return jnp.where(takes_long(piece), long_lane, lane)

    def near_slot(index):
        return 2 * index + core

    def cross_slot(index):
        return 2 * index + 1 - core

    def cross_at(y_here):
        free = jnp.where(q <= 1, 1, jnp.where(q >= 5, 0, core))
        return jnp.where(y_here == core, free, core)

    crossed = cross_at(y)
    pass_lane = 2 * crossed - 1
    cross_as = cross_at(1 - y)
    cross_of = 1 - y + cross_as - core

    first = jnp.where(odd, 1, jnp.where(z == 0, 0, jnp.where(z == 6, 2, 2 * core)))
    right_own = (z + first) % 8 == 0
    second = jnp.where(odd, 2 - 2 * half, 2 - first)
    third = 3 - first - second

    def own_slot(index):
        return (2 * index - y + 5) % 5

    def shared_slot(index):
        return 2 * (index + core) + 1 - 2 * core - y

    hop = 1 - 2 * half
    send1_to = q + jnp.where(odd, hop, 2 * first - 2)
    send1_as = jnp.where(odd, 1 - hop, 2 - first)
    send2_of = jnp.where(odd, second, 2 - 2 * half)
    send2_to = q + jnp.where(odd, 2 * hop, hop)
    send2_as = jnp.where(odd, third, 1)

    barrier = pltpu.get_barrier_semaphore()

    def greet(device):
        pl.semaphore_signal(barrier, inc=1, device_id=device, device_id_type=MESH)

    @pl.when(jnp.logical_not(left_own))
    def _():
        greet(at(q, z + skew, y, core))

    greet(at(q, z - lane, y, core))

    @pl.when(relays)
    def _():
        greet(at(q, z - long_lane, y, core))
        greet(at(q, z - long_lane * (long_way - 2), y, core))
        greet(at(q, z - long_lane * 2, y, core))

    greet(at(q, z, 1 - y, core))
    greet(at(q, z - pass_lane, y, core))

    @pl.when(jnp.logical_not(right_own))
    def _():
        greet(at(q + z + first, z, y, core))

    greet(at(q + jnp.where(odd, hop, 2 - 2 * first), z, y, core))
    greet(at(q + jnp.where(odd, -2 * hop, hop), z, y, core))
    greet(at(q, z, y, 1 - core))

    absent = left_own.astype(jnp.int32) + right_own.astype(jnp.int32)
    pl.semaphore_wait(barrier, 8 - absent + jnp.where(relays, 3, 0))

    def rows(piece):
        return pl.ds(piece * PIECE_ROWS, PIECE_ROWS)

    def own_part(piece):
        return cols_hbm if piece == COLS else data_hbm.at[rows(piece)]

    def left_part(slot, piece):
        return left_cols.at[slot] if piece == COLS else left.at[slot, rows(piece)]

    def right_part(slot, piece):
        return right_cols.at[slot] if piece == COLS else right.at[slot, rows(piece)]

    def move(source, target, kind, piece, sem, device):
        return pltpu.make_async_remote_copy(
            src_ref=source,
            dst_ref=target,
            send_sem=send_sem.at[kind, piece],
            recv_sem=sem,
            device_id=device,
            device_id_type=MESH,
        )

    def to_left(source, slot, kind, piece, device):
        return move(source, left_part(slot, piece), kind, piece, left_sem.at[slot, piece], device)

    def to_right(source, slot, kind, piece, device):
        return move(source, right_part(slot, piece), kind, piece, right_sem.at[slot, piece], device)

    def left_skew(piece):
        return to_left(own_part(piece), near_slot(land), 0, piece, at(q, z - skew, y, core))

    def left_long(piece):
        device = at(q, z + long_lane * (long_way - 2), y, core)
        return move(own_part(piece), relay.at[piece], 0, piece, relay_sem.at[piece], device)

    def left_relay(piece):
        return to_left(relay.at[piece], near_slot(1 - land), 10, piece, at(q, z + long_lane * 2, y, core))

    def left_next(piece):
        here, there = near_slot(land_of(piece)), near_slot(1 - land_of(piece))
        return to_left(left_part(here, piece), there, 1, piece, at(q, z + lane_of(piece), y, core))

    def left_cross(piece):
        return to_left(left_part(near_slot(cross_of), piece), cross_slot(cross_as), 2, piece, at(q, z, 1 - y, core))

    def left_pass(piece):
        source = left_part(cross_slot(crossed), piece)
        return to_left(source, cross_slot(1 - crossed), 3, piece, at(q, z + pass_lane, y, core))

    def right_skew(piece):
        return to_right(own_part(piece), own_slot(first), 4, piece, at(q - z - first, z, y, core))

    def right_send1(piece):
        return to_right(right_part(own_slot(first), piece), own_slot(send1_as), 5, piece, at(send1_to, z, y, core))

    def right_send2(piece):
        return to_right(right_part(own_slot(send2_of), piece), own_slot(send2_as), 6, piece, at(send2_to, z, y, core))

    def right_share(index, kind, piece):
        slot = 2 * index - 1 + 2 * core - y
        return to_right(right_part(own_slot(index), piece), slot, kind, piece, at(q, z, y, 1 - core))

    def left_here(slot, piece):
        to_left(left_part(slot, piece), slot, 0, piece, at(q, z, 1 - y, core)).wait_recv()

    def right_here(slot, piece):
        to_right(right_part(slot, piece), slot, 0, piece, at(q, z, 1 - y, core)).wait_recv()

    def keep_left(piece):
        return pltpu.make_async_copy(own_part(piece), left_part(near_slot(land), piece), keep_sem.at[0, piece])

    def keep_right(piece):
        return pltpu.make_async_copy(own_part(piece), right_part(own_slot(first), piece), keep_sem.at[1, piece])

    def shares(index):
        return index != 2 * core

    side = lax.broadcasted_iota(jnp.int32, (BS, 128), 1) // BS

    def spread(slot, piece):
        def one(index, carry):
            inner = piece * PIECE_BLOCKS + index
            here = pl.ds(pl.multiple_of(inner * BS, BS), BS)
            block = right[slot, here, :]
            top = block.astype(jnp.bfloat16)
            rest = (block - top.astype(jnp.float32)).astype(jnp.bfloat16)
            targets = [right_at[slot, place, inner] for place in range(4)]
            for value, kept in ((top, high), (rest, low)):
                doubled = []
                for pair in range(2):
                    both = value[:, pair * 128 : pair * 128 + 128]
                    even, uneven = both[:, :BS], both[:, BS:]
                    doubled.append(jnp.concatenate([even, even], axis=1))
                    doubled.append(jnp.concatenate([uneven, uneven], axis=1))
                for group in range(8):
                    spot = side + 2 * group
                    result = jnp.zeros((BS, 128), jnp.bfloat16)
                    for place in range(4):
                        result = jnp.where(spot == targets[place], doubled[place], result)
                    kept[slot, inner, :, group * 128 : group * 128 + 128] = result
            return carry

        lax.fori_loop(0, PIECE_BLOCKS, one, 0)

    def right_ready(slot, piece):
        if piece == COLS:
            copy = pltpu.make_async_copy(right_cols.at[slot], right_at.at[slot], at_sem)
            copy.start()
            copy.wait()
        else:
            spread(slot, piece)

    def own_ready(index, piece):
        @pl.when(own_slot(index) < 4)
        def _():
            right_ready(own_slot(index), piece)

    def products(piece, slots, fresh):
        def one(index, carry):
            block_row = piece * PIECE_BLOCKS + index
            here = pl.ds(pl.multiple_of(block_row * BS, BS), BS)
            place = lax.broadcasted_iota(jnp.int32, (BS, 256), 1) // BS
            tops, rests, starts = [], [], []
            for step in slots:
                used = jnp.zeros((BS, 256), jnp.bool_)
                for slot in range(4):
                    inner = left_at[step, slot, block_row]
                    used = used | (place == jnp.where(inner >= 0, slot, -1))
                    starts.append((step, jnp.maximum(inner, 0)))
                block = jnp.where(used, left[step, here, :], 0.0)
                top = block.astype(jnp.bfloat16)
                tops.append(top)
                rests.append((block - top.astype(jnp.float32)).astype(jnp.bfloat16))
            top = jnp.concatenate(tops, axis=1)
            both = jnp.concatenate([top, jnp.concatenate(rests, axis=1)], axis=0)
            for quarter in range(4):
                lanes = slice(quarter * 256, quarter * 256 + 256)
                right_top = jnp.concatenate([high[step, start, :, lanes] for step, start in starts], axis=0)
                right_rest = jnp.concatenate([low[step, start, :, lanes] for step, start in starts], axis=0)
                main = jnp.dot(both, right_top, preferred_element_type=jnp.float32)
                extra = jnp.dot(top, right_rest, preferred_element_type=jnp.float32)
                term = main[:BS] + main[BS:] + extra
                out[here, lanes] = term if fresh else out[here, lanes] + term
            return carry

        lax.fori_loop(0, PIECE_BLOCKS, one, 0)

    def write(piece):
        return pltpu.make_async_copy(out.at[rows(piece)], out_hbm.at[rows(piece)], out_sem.at[piece])

    def left_start(piece):
        @pl.when(left_own)
        def _():
            keep_left(piece).start()

        @pl.when(jnp.logical_not(left_own | takes_long(piece)))
        def _():
            left_skew(piece).start()

        if piece != COLS:
            @pl.when(takes_long(piece))
            def _():
                left_long(piece).start()

    def right_start(piece):
        @pl.when(right_own)
        def _():
            keep_right(piece).start()

        @pl.when(jnp.logical_not(right_own))
        def _():
            right_skew(piece).start()

    def start_after(start, piece, ahead):
        place = ALL.index(piece) + ahead
        if place < len(ALL):
            start(ALL[place])

    for piece in ALL[:RIGHT_AHEAD]:
        right_start(piece)
    for piece in ALL[:LEFT_AHEAD]:
        left_start(piece)

    def right_first(piece):
        @pl.when(right_own)
        def _():
            keep_right(piece).wait()

        @pl.when(jnp.logical_not(right_own))
        def _():
            right_here(own_slot(first), piece)

        right_send1(piece).start()

        @pl.when(shares(first))
        def _():
            right_share(first, 7, piece).start()

    def right_second(piece):
        right_here(own_slot(second), piece)
        right_send2(piece).start()

        @pl.when(shares(second))
        def _():
            right_share(second, 8, piece).start()

    def right_third(piece):
        right_here(own_slot(third), piece)

        @pl.when(shares(third))
        def _():
            right_share(third, 9, piece).start()

    def left_first(piece):
        @pl.when(left_own)
        def _():
            keep_left(piece).wait()

        @pl.when(jnp.logical_not(left_own))
        def _():
            left_here(near_slot(land_of(piece)), piece)

        left_next(piece).start()

        @pl.when(cross_of == land_of(piece))
        def _():
            left_cross(piece).start()

    def left_second(piece):
        left_here(near_slot(1 - land_of(piece)), piece)

        @pl.when(cross_of != land_of(piece))
        def _():
            left_cross(piece).start()

    def left_third(piece):
        left_here(cross_slot(crossed), piece)
        left_pass(piece).start()

    def left_last(piece):
        left_here(cross_slot(1 - crossed), piece)

    def relayed(piece):
        if piece != COLS:
            @pl.when(takes_long(piece))
            def _():
                move(relay.at[piece], relay.at[piece], 0, piece, relay_sem.at[piece], at(q, z, 1 - y, core)).wait_recv()
                left_relay(piece).start()

    def right_landed(piece):
        right_first(piece)
        start_after(right_start, piece, RIGHT_AHEAD)
        own_ready(first, piece)

    def right_followed(piece):
        right_second(piece)
        own_ready(second, piece)

    def right_finished(piece):
        right_third(piece)
        own_ready(third, piece)

    def right_shared(piece):
        for index in range(2):
            right_here(shared_slot(index), piece)
            right_ready(shared_slot(index), piece)

    def left_landed(piece):
        left_first(piece)
        start_after(left_start, piece, LEFT_AHEAD)

    def left_ended(piece):
        left_last(piece)
        if piece == COLS:
            copy = pltpu.make_async_copy(left_cols, left_at, at_sem)
            copy.start()
            copy.wait()

    def near_products(piece):
        products(piece, (near_slot(0), near_slot(1)), True)

    def crossed_products(piece):
        products(piece, (cross_slot(crossed),), False)

    def last_products(piece):
        products(piece, (cross_slot(1 - crossed),), False)
        write(piece).start()

    events = []
    for place, piece in enumerate(ALL):
        right_turn, left_turn = place * RIGHT_PACE, place + 0.3
        for lag, stage in enumerate((right_landed, right_followed, right_finished, right_shared)):
            events.append((right_turn + lag * RIGHT_LAG, stage, piece))
        for lag, stage in enumerate((relayed, left_landed, left_second, left_third)):
            events.append((left_turn + (lag - 0.5) * LEFT_LAG, stage, piece))
        events.append((left_turn + 2.5 * LEFT_LAG + END_LAG, left_ended, piece))
    ready = max(turn for turn, stage, piece in events if stage is right_shared)
    at_turn = {(stage, piece): turn for turn, stage, piece in events}
    cols_turn = at_turn[left_ended, COLS]
    for place, piece in enumerate(ALL[1:]):
        least = max(ready, cols_turn) + 0.01 + SPACING * place
        events.append((max(least, at_turn[left_second, piece] + 0.01), near_products, piece))
        events.append((max(least + 0.05, at_turn[left_third, piece] + 0.02), crossed_products, piece))
        events.append((max(least + 0.1, at_turn[left_ended, piece] + 0.01), last_products, piece))
    for turn, stage, piece in sorted(events, key=lambda event: event[0]):
        stage(piece)

    for piece in ALL:
        @pl.when(jnp.logical_not(left_own))
        def _():
            left_skew(piece).wait_send()

        @pl.when(jnp.logical_not(right_own))
        def _():
            right_skew(piece).wait_send()

        if piece != COLS:
            @pl.when(takes_long(piece))
            def _():
                left_relay(piece).wait_send()

        left_next(piece).wait_send()
        left_cross(piece).wait_send()
        left_pass(piece).wait_send()
        right_send1(piece).wait_send()
        right_send2(piece).wait_send()
        for index, kind in ((first, 7), (second, 8), (third, 9)):
            @pl.when(shares(index))
            def _():
                right_share(index, kind, piece).wait_send()

        if piece != COLS:
            write(piece).wait()


def deliver_kernel(result_ref, out_ref, sem):
    copies = []
    for index in range(8):
        rows = pl.ds(index * 128, 128)
        copies.append(pltpu.make_async_copy(result_ref.at[rows], out_ref.at[rows], sem.at[index]))
        copies[-1].start()
    for copy in copies:
        copy.wait()


def deliver(result):
    return pl.pallas_call(
        deliver_kernel,
        out_shape=jax.ShapeDtypeStruct(result.shape, result.dtype),
        in_specs=[pl.BlockSpec(memory_space=pl.ANY)],
        out_specs=pl.BlockSpec(memory_space=pl.ANY),
        scratch_shapes=[
            pltpu.SemaphoreType.DMA((8,)),
        ],
        compiler_params=pltpu.CompilerParams(vmem_limit_bytes=16 * 2**20),
        name="deliver",
    )(result)


def local(p_cols, p_data):
    count = len(ALL)
    result = pl.pallas_call(
        kernel,
        out_shape=jax.ShapeDtypeStruct((1024, 1024), jnp.float32),
        in_specs=[pl.BlockSpec(memory_space=pltpu.HBM)] * 2,
        out_specs=pl.BlockSpec(memory_space=pl.ANY),
        scratch_shapes=[
            pltpu.VMEM((4, 1024, 256), jnp.float32),
            pltpu.VMEM((4, 4, 16), jnp.int32),
            pltpu.VMEM((5, 1024, 256), jnp.float32),
            pltpu.VMEM((5, 4, 16), jnp.int32),
            pltpu.VMEM((PIECES, PIECE_ROWS, 256), jnp.float32),
            pltpu.VMEM((STEPS, 16, BS, 1024), jnp.bfloat16),
            pltpu.VMEM((STEPS, 16, BS, 1024), jnp.bfloat16),
            pltpu.VMEM((1024, 1024), jnp.float32),
            pltpu.SMEM((4, 4, 16), jnp.int32),
            pltpu.SMEM((4, 4, 16), jnp.int32),
            pltpu.SemaphoreType.DMA((2, count)),
            pltpu.SemaphoreType.DMA((11, count)),
            pltpu.SemaphoreType.DMA((4, count)),
            pltpu.SemaphoreType.DMA((5, count)),
            pltpu.SemaphoreType.DMA((PIECES,)),
            pltpu.SemaphoreType.DMA,
            pltpu.SemaphoreType.DMA((PIECES,)),
        ],
        compiler_params=pltpu.CompilerParams(
            collective_id=0, has_side_effects=True, vmem_limit_bytes=36 * 2**20
        ),
        name="window_square",
    )(p_cols.T, p_data)
    return deliver(result)


def solution(mesh):
    return jax.shard_map(
        local, mesh=mesh, in_specs=(P("row", "col"), P("row", "col")), out_specs=P("row", "col"), check_vma=False
    )
```
